32 devices in a mesh: blk: 8 (over y, x, core), head: 4 (over z).
Axes of the slice: x: 2, y: 2, z: 4, core: 2. Of those that a mesh axis runs over, the one named last changes fastest.
Arguments:
- hidden_in: bfloat16 [2, 2048, 768], P(None, ('blk', 'head')), may hold values from -6 to 6
- cotangent: bfloat16 [2, 2048, 768], P(None, ('blk', 'head')), may hold values from -6 to 6
- lengths: int32 [2], replicated, may hold values from 512 to 2048, as said below
- w_query: bfloat16 [768, 768], P(('blk', 'head')), may hold values from -0.21875 to 0.21875
- b_query: bfloat16 [768], P(('blk', 'head')), may hold values from -4 to 4
- w_key: bfloat16 [768, 768], P(('blk', 'head')), may hold values from -0.21875 to 0.21875
- w_value: bfloat16 [768, 768], P(('blk', 'head')), may hold values from -0.21875 to 0.21875
- b_value: bfloat16 [768], P(('blk', 'head')), may hold values from -0.3125 to 0.3125
- w_out: bfloat16 [768, 768], P(('blk', 'head')), may hold values from -4 to 4
- b_out: bfloat16 [768], P(('blk', 'head')), may hold values from -4 to 4
- gain_one: bfloat16 [768], P(('blk', 'head')), may hold values from 0.5 to 1.5
- shift_one: bfloat16 [768], P(('blk', 'head')), may hold values from -3 to 3
- w_up: bfloat16 [768, 3072], P(('blk', 'head')), may hold values from -0.21875 to 0.21875
- b_up: bfloat16 [3072], P(('blk', 'head')), may hold values from -6 to 6
- w_down: bfloat16 [3072, 768], P(('blk', 'head')), may hold values from -0.109375 to 0.109375
- b_down: bfloat16 [768], P(('blk', 'head')), may hold values from -4 to 4
- gain_two: bfloat16 [768], P(('blk', 'head')), may hold values from 0.5 to 1.5
- shift_two: bfloat16 [768], P(('blk', 'head')), may hold values from -3 to 3
Outputs:
- output: bfloat16 [2, 2048, 768], P(None, ('blk', 'head'))
- grad_input: float32 [2, 2048, 768], P(None, ('blk', 'head'))
- grad_w_query: float32 [768, 768], P(('blk', 'head'))
- grad_b_query: float32 [768], P(('blk', 'head'))
- grad_w_key: float32 [768, 768], P(('blk', 'head'))
- grad_w_value: float32 [768, 768], P(('blk', 'head'))
- grad_b_value: float32 [768], P(('blk', 'head'))
- grad_w_out: float32 [768, 768], P(('blk', 'head'))
- grad_b_out: float32 [768], P(('blk', 'head'))
- grad_gain_one: float32 [768], P(('blk', 'head'))
- grad_shift_one: float32 [768], P(('blk', 'head'))
- grad_w_up: float32 [768, 3072], P(('blk', 'head'))
- grad_b_up: float32 [3072], P(('blk', 'head'))
- grad_w_down: float32 [3072, 768], P(('blk', 'head'))
- grad_b_down: float32 [768], P(('blk', 'head'))
- grad_gain_two: float32 [768], P(('blk', 'head'))
- grad_shift_two: float32 [768], P(('blk', 'head'))
The draws below stay inside these ranges and needn't reach their ends.
Inputs may be any that keep to these rules, and one draw needn't show every extreme that they name: `lengths`: each length lies in 512 to 2048, and at least one sequence is full.
All inputs are finite; a program needn't handle non-finite values.
Results may differ from the reference program's by a relative error of at most 0.023.
Values may be sent and summed in bfloat16 or wider, within the bound.
A program may use at most 192 MiB of HBM per device.

```python
import jax
import jax.numpy as jnp
from jax import lax

D = 768
HEADS = 12
HEAD_DIM = 64
FF = 3072
SEQS = 2
LEN = 2048


def draw_lengths(key, part):
    drawn = jax.random.randint(jax.random.fold_in(key, 11), (SEQS,), LEN // 4, LEN + 1)
    chosen = jax.random.randint(jax.random.fold_in(key, 12), (), 0, SEQS)
    return jnp.where(jnp.arange(SEQS) == chosen, LEN, drawn).astype(jnp.int32)


def block_levels(own_key, extent, split, smallest, top_value):
    def one(dim, blocks):
        steps = jax.random.uniform(jax.random.fold_in(jax.random.fold_in(own_key, 6), dim), (blocks,), jnp.float32, smallest / len(split), top_value / len(split))
        return jnp.repeat(jnp.exp(steps), extent[dim] // blocks).reshape((-1,) + (1,) * (len(extent) - dim - 1))

    factor_of = one(*split[0])
    for cut in split[1:]:
        factor_of = factor_of * one(*cut)
    return factor_of


def gaussian(own_key, extent, deviation, most, pieces=(), kind=jnp.bfloat16):
    values = jax.random.normal(own_key, extent, jnp.float32) * deviation
    if len(pieces) > 0:
        values = block_levels(own_key, extent, pieces, -0.22, 0.18) * values
    return jnp.clip(values, min=-most, max=most).astype(kind)


def setup_inputs(seed: int = 0) -> dict:
    arg_keys = jax.random.split(jax.random.key(seed), 19)
    hidden_in = gaussian(arg_keys[0], (SEQS, LEN, D), 1.0, 6.0, ((1, 32),))
    cotangent = gaussian(arg_keys[1], (SEQS, LEN, D), 1.0, 6.0, ((1, 32),))
    lengths = draw_lengths(jax.random.fold_in(arg_keys[18], 71), 0)
    w_query = gaussian(arg_keys[3], (D, D), D ** -0.5, 0.21875, ((0, 32),))
    b_query = gaussian(arg_keys[4], (D,), 0.3, 4.0, ((0, 32),))
    w_key = gaussian(arg_keys[5], (D, D), D ** -0.5, 0.21875, ((0, 32),))
    w_value = gaussian(arg_keys[6], (D, D), D ** -0.5, 0.21875, ((0, 32),))
    b_value = gaussian(arg_keys[7], (D,), 0.02, 0.3125, ((0, 32),))
    w_out = gaussian(arg_keys[8], (D, D), 2 ** -0.5, 4.0, ((0, 32),))
    b_out = gaussian(arg_keys[9], (D,), 0.3, 4.0, ((0, 32),))
    gain_one = jnp.clip(1.0 + 0.1 * jax.random.normal(arg_keys[10], (D,), jnp.float32), 0.5, 1.5).astype(jnp.bfloat16)
    shift_one = gaussian(arg_keys[11], (D,), 0.2, 3.0, ((0, 32),))
    w_up = gaussian(arg_keys[12], (D, FF), D ** -0.5, 0.21875, ((0, 32),))
    b_up = gaussian(arg_keys[13], (FF,), 0.5, 6.0, ((0, 32),))
    w_down = gaussian(arg_keys[14], (FF, D), FF ** -0.5, 0.109375, ((0, 32),))
    b_down = gaussian(arg_keys[15], (D,), 0.3, 4.0, ((0, 32),))
    gain_two = jnp.clip(1.0 + 0.1 * jax.random.normal(arg_keys[16], (D,), jnp.float32), 0.5, 1.5).astype(jnp.bfloat16)
    shift_two = gaussian(arg_keys[17], (D,), 0.2, 3.0, ((0, 32),))
    return {"hidden_in": hidden_in, "cotangent": cotangent, "lengths": lengths, "w_query": w_query, "b_query": b_query, "w_key": w_key, "w_value": w_value, "b_value": b_value, "w_out": w_out, "b_out": b_out, "gain_one": gain_one, "shift_one": shift_one, "w_up": w_up, "b_up": b_up, "w_down": w_down, "b_down": b_down, "gain_two": gain_two, "shift_two": shift_two}


@jax.custom_vjp
def low(v):
    return lax.optimization_barrier(v.astype(jnp.bfloat16)).astype(jnp.float32)

@jax.custom_vjp
def low_back(v):
    return v

def low_keep(v):
    return (low(v), None)

def low_pass(kept, grad):
    return (grad,)

def back_keep(v):
    return (v, None)

def back_low(kept, grad):
    return (low(grad),)
low.defvjp(low_keep, low_pass)
low_back.defvjp(back_keep, back_low)
highest = lax.Precision.HIGHEST
norm_eps = 1e-06

def layer_norm(entries, norm_gain, norm_shift):
    average = lax.optimization_barrier(jnp.mean(entries, axis=-1, keepdims=True))
    centred = entries - average
    spread = lax.optimization_barrier(jnp.mean(centred * centred, axis=-1, keepdims=True))
    return centred * lax.rsqrt(spread + norm_eps) * norm_gain + norm_shift

def product(left, right):
    return jnp.dot(left, right, precision=highest, preferred_element_type=jnp.float32)

def attention(queries, keys, values, lengths):
    block_rows = min(256, LEN)
    blocks_per = LEN // block_rows
    positions = jnp.arange(LEN, dtype=jnp.int32)

    def one_block(flat_index):
        which_seq = (flat_index // blocks_per).astype(jnp.int32)
        which_block = (flat_index % blocks_per).astype(jnp.int32)
        zero_index = jnp.zeros((), jnp.int32)
        query_block = lax.dynamic_slice(queries, (which_seq, which_block * block_rows, zero_index, zero_index), (1, block_rows, HEADS, HEAD_DIM))[0]
        key_seq = lax.dynamic_index_in_dim(keys, which_seq, 0, keepdims=False)
        value_seq = lax.dynamic_index_in_dim(values, which_seq, 0, keepdims=False)
        limit = lax.dynamic_index_in_dim(lengths, which_seq, 0, keepdims=False)
        valid = positions < limit
        scores = low_back(jnp.einsum('qhd,khd->hqk', query_block, key_seq, precision=highest) * HEAD_DIM ** (-0.5))
        scores = jnp.where(valid[None, None, :], scores, -1e+30)
        top_score = lax.optimization_barrier(jnp.max(scores, axis=-1, keepdims=True))
        weights = jnp.exp(scores - top_score)
        weights = weights / lax.optimization_barrier(jnp.sum(weights, axis=-1, keepdims=True))
        return jnp.einsum('hqk,khd->qhd', low(weights), value_seq, precision=highest)
    blocks = lax.map(jax.checkpoint(one_block), jnp.arange(SEQS * blocks_per, dtype=jnp.int32))
    return blocks.reshape(SEQS, LEN, HEADS * HEAD_DIM)

def reference(hidden_in, cotangent, lengths, w_query, b_query, w_key, w_value, b_value, w_out, b_out, gain_one, shift_one, w_up, b_up, w_down, b_down, gain_two, shift_two):

    def forward(inputs, query_mat, query_bias, key_mat, value_mat, value_bias, out_mat, out_bias, gain_first, shift_first, up_mat, up_bias, down_mat, down_bias, gain_second, shift_second):
        rows = inputs.reshape(SEQS * LEN, D)
        queries = low_back(low(product(rows, query_mat) + query_bias))
        keys = low_back(low(product(rows, key_mat)))
        values = low_back(low(product(rows, value_mat) + value_bias))
        shape_four = (SEQS, LEN, HEADS, HEAD_DIM)
        mixed = attention(queries.reshape(shape_four), keys.reshape(shape_four), values.reshape(shape_four), lengths)
        mixed = low_back(low(mixed.reshape(SEQS * LEN, D)))
        branch = low_back(product(mixed, out_mat) + out_bias)
        normed = low(layer_norm(rows + branch, gain_first, shift_first))
        up_pre = low_back(product(normed, up_mat) + up_bias)
        activated = low(jax.nn.gelu(up_pre, approximate=False))
        second = low_back(product(activated, down_mat) + down_bias)
        result = layer_norm(normed + second, gain_second, shift_second)
        return result.reshape(SEQS, LEN, D)
    params = (w_query, b_query, w_key, w_value, b_value, w_out, b_out, gain_one, shift_one, w_up, b_up, w_down, b_down, gain_two, shift_two)
    params = tuple((entry.astype(jnp.float32) for entry in params))
    result, backward = jax.vjp(forward, hidden_in.astype(jnp.float32), *params)
    row_valid = (jnp.arange(LEN, dtype=jnp.int32)[None, :] < lengths[:, None]).astype(jnp.float32)
    grads = backward(cotangent.astype(jnp.float32) * row_valid[:, :, None])
    return (result.astype(jnp.bfloat16), grads[0], grads[1], grads[2], grads[3], grads[4], grads[5], grads[6], grads[7], grads[8], grads[9], grads[10], grads[11], grads[12], grads[13], grads[14], grads[15])
```

```python
import functools

import jax
import jax.numpy as jnp
import numpy as np
from jax import lax
from jax.experimental import pallas as pl
from jax.experimental.pallas import tpu as pltpu
from jax.sharding import PartitionSpec as P

HEAD_DIM = 64
norm_eps = 1e-06
neg_big = -1e30
MESH = pl.DeviceIdType.MESH
f32 = jnp.float32
bf16 = jnp.bfloat16


def dot(a, b, ca, cb):
    return lax.dot_general(a, b, (((ca,), (cb,)), ((), ())), preferred_element_type=f32)


def span(bits):
    out = [0]
    for bit in bits:
        out = out + [m ^ (1 << bit) for m in out]
    return out


class Links:
    def __init__(self, blocks, zs, send, recv):
        self.B, self.Z = blocks, zs
        self.b = lax.axis_index("blk")
        self.z = lax.axis_index("head")
        self.send, self.recv, self.used = send, recv, 0

    def take(self, count):
        base = self.used
        self.used += count
        return base

    def at(self, axis):
        if axis == "blk":
            return self.b, lambda i: (i, self.z)
        return self.z, lambda i: (self.b, i)

    def copy(self, src, dst, sem, bt, zt):
        return pltpu.make_async_remote_copy(
            src_ref=src, dst_ref=dst, send_sem=self.send.at[sem], recv_sem=self.recv.at[sem],
            device_id=(bt, zt), device_id_type=MESH,
        )


def bit_tree(order):
    pos = {bit: i for i, bit in enumerate(order)}
    rows = []
    for m in span(order):
        last = max([pos[bit] for bit in order if m >> bit & 1], default=-1)
        over = order[last] if last >= 0 else None
        rows.append((bin(m).count("1"), last, m, over, [bit for bit in order if pos[bit] > last]))
    rows.sort(key=lambda r: (0 if r[4] else 1, r[0], r[1]))
    return [(m, over, onward) for _, _, m, over, onward in rows]


def bit_gather(L, get, order, own=None, mask0=0, guard=None, axis="blk"):
    base = L.take(1 << max(order, default=0) + 1)
    b, to = L.at(axis)
    turn = (lambda f: f()) if guard is None else pl.when(guard)

    def out(m, over):
        blk = b ^ (m ^ (1 << over)) ^ mask0
        src = own if own is not None and m == 1 << over else get(blk)
        return L.copy(src, get(blk), base + m, *to(b ^ (1 << over)))

    tree = bit_tree(order)
    for m, over, onward in tree:
        if m:
            yield

        @turn
        def _():
            if m:
                L.copy(get(b ^ m ^ mask0), get(b ^ m ^ mask0), base + m, *to(b ^ (1 << over))).wait_recv()
            for bit in onward:
                out(m ^ (1 << bit), bit).start()

    yield

    @turn
    def _():
        for m, over, onward in tree:
            if m:
                out(m, over).wait_send()


def bit_reduce(L, get, slot, order, add, mask0=0, axis="blk"):
    base = L.take(1 << max(order, default=0) + 1)
    b, to = L.at(axis)
    tree = bit_tree(order)
    pos = {bit: i for i, bit in enumerate(order)}

    def out(m, over):
        return L.copy(get(b ^ m ^ mask0), slot(m), base + m, *to(b ^ (1 << over)))

    steps = sorted((row for row in tree if row[0]), key=lambda r: (-pos[r[1]], -bin(r[0]).count("1")))
    waiting = {m: len(onward) for m, _, onward in tree}
    overs = {m: over for m, over, _ in tree}
    for m, over, onward in steps:
        if not onward:
            out(m, over).start()
    for m, over, onward in steps:
        yield
        out(m, over).wait_recv()
        parent = m ^ (1 << over)
        add(get(b ^ parent ^ mask0), slot(m))
        waiting[parent] -= 1
        if waiting[parent] == 0 and parent:
            out(parent, overs[parent]).start()
    yield
    for m, over, onward in steps:
        out(m, over).wait_send()


def line_gather(L, get, own=None):
    b, z, Z = L.b, L.z, L.Z
    base = {1: L.take(Z), -1: L.take(Z)}

    def hop(zi, dist, way):
        src = own if own is not None and dist == 1 else get(zi)
        return L.copy(src, get(zi), base[way] + dist, b, z + way)

    def room(way):
        return z < Z - 1 if way > 0 else z > 0

    def exists(dist, way):
        return z >= dist if way > 0 else z + dist < Z

    for way in (1, -1):
        pl.when(room(way))(lambda way=way: hop(z, 1, way).start())
    for dist in range(1, Z):
        yield
        for way in (1, -1):

            @pl.when(exists(dist, way))
            def _():
                L.copy(get(z - way * dist), get(z - way * dist), base[way] + dist, b, z - way).wait_recv()

            if dist < Z - 1:
                pl.when(exists(dist, way) & room(way))(
                    lambda way=way: hop(z - way * dist, dist + 1, way).start()
                )
    yield
    for dist in range(1, Z):
        for way in (1, -1):
            pl.when(exists(dist - 1, way) & room(way))(
                lambda way=way: hop(z - way * (dist - 1), dist, way).wait_send()
            )


def line_reduce(L, get, slot, add):
    b, z, Z = L.b, L.z, L.Z
    base = {1: L.take(Z), -1: L.take(Z)}

    def hop(zi, way):
        return L.copy(get(zi), slot(way, zi), base[way] + zi, b, z + way)

    for j in range(Z - 1):
        for way in (1, -1):
            zi = Z - 1 - j if way > 0 else j
            took = (z > 0) & (z <= zi) if way > 0 else (z < Z - 1) & (z >= zi)
            gives = z < zi if way > 0 else z > zi
            if j > 0 or Z > 1:
                yield

            @pl.when(took)
            def _(zi=zi, way=way):
                L.copy(get(zi), slot(way, zi), base[way] + zi, b, z - way).wait_recv()
                add(get(zi), slot(way, zi))

            pl.when(gives)(lambda zi=zi, way=way: hop(zi, way).start())
    yield
    for j in range(Z - 1):
        for way in (1, -1):
            zi = Z - 1 - j if way > 0 else j
            gives = z < zi if way > 0 else z > zi
            pl.when(gives)(lambda zi=zi, way=way: hop(zi, way).wait_send())


def line_swap(L, src, dst):
    b, z, Z = L.b, L.z, L.Z
    base = L.take(Z)

    def out(k):
        zt = lax.rem(z + k, Z)
        return L.copy(src(zt), dst(z), base + k, b, zt)

    for k in range(1, Z):
        out(k).start()
    yield
    for k in range(1, Z):
        zs = lax.rem(z + Z - k, Z)
        L.copy(src(zs), dst(zs), base + k, b, zs).wait_recv()
    yield
    for k in range(1, Z):
        out(k).wait_send()


def wide_gather(L, one, many, own, order):
    at = order.index("z")
    pre, post = order[:at], order[at + 1 :]
    b, z = L.b, L.z
    lines = []
    tree = bit_tree(pre)
    base = L.take(1 << max(pre, default=0) + 1)

    def out(m, over):
        blk = b ^ (m ^ (1 << over))
        src = own if m == 1 << over else one(blk, z)
        return L.copy(src, one(blk, z), base + m, b ^ (1 << over), z)

    for m, over, onward in tree:
        if m:
            yield
            L.copy(one(b ^ m, z), one(b ^ m, z), base + m, b ^ (1 << over), z).wait_recv()
        for bit in onward:
            out(m ^ (1 << bit), bit).start()
        line = line_gather(L, lambda zi, m=m: one(b ^ m, zi), own if m == 0 else None)
        next(line)
        lines.append((m, line))
    ends = []
    trees = []
    for dist in range(1, L.Z):
        for m, line in lines:
            yield
            next(line)
            if dist == L.Z - 1:
                t = bit_gather(L, many, post, mask0=m)
                if post:
                    next(t)
                trees.append(t)
    yield
    for step in range((1 << len(post)) - 1):
        for t in trees:
            next(t)
            yield
    for t in trees:
        for _ in t:
            pass
    for m, line in lines:
        for _ in line:
            pass
    for m, over, onward in tree:
        if m:
            out(m, over).wait_send()


def blk_swap(L, src, dst):
    b, z, B = L.b, L.z, L.B
    base = L.take(B)

    def out(k):
        return L.copy(src(b ^ k), dst(b), base + k, b ^ k, z)

    for k in range(1, B):
        out(k).start()
    yield
    for k in range(1, B):
        L.copy(src(b ^ k), dst(b ^ k), base + k, b ^ k, z).wait_recv()
    yield
    for k in range(1, B):
        out(k).wait_send()


def add_rows(dst, src, step):
    rows = dst.shape[0]

    def one(r, carry):
        at = pl.ds(pl.multiple_of(r * step, step), step)
        dst[at] = (dst[at].astype(f32) + src[at].astype(f32)).astype(dst.dtype)
        return carry

    if rows == step:
        dst[...] = (dst[...].astype(f32) + src[...].astype(f32)).astype(dst.dtype)
    else:
        lax.fori_loop(0, rows // step, one, 0)


def pump(jobs, turns=1):
    for _ in range(turns):
        for job in list(jobs):
            if next(job, 0) == 0:
                jobs.remove(job)


def drain(jobs):
    while jobs:
        pump(jobs)


def normed(entries):
    average = jnp.mean(entries, axis=-1, keepdims=True)
    centred = entries - average
    scale = lax.rsqrt(jnp.mean(centred * centred, axis=-1, keepdims=True) + norm_eps)
    return centred * scale, scale


def norm_back(grad, gain, unit, scale):
    inner = grad * gain
    return scale * (
        inner - jnp.mean(inner, axis=-1, keepdims=True) - unit * jnp.mean(inner * unit, axis=-1, keepdims=True)
    )


class Plan:
    def __init__(self, B, Z, seqs, tokens, width, hidden):
        self.B, self.Z, self.S, self.T, self.D, self.F = B, Z, seqs, tokens, width, hidden
        self.rows = seqs * tokens
        self.Tq = tokens * Z
        self.R = self.rows * Z
        self.LK = self.Tq * B
        self.Dh = width // Z
        self.heads = self.Dh // HEAD_DIM
        self.wide = -(-3 * self.Dh // 128) * 128
        self.Fb = hidden // B
        self.rd = width // (B * Z)
        self.rf = hidden // (B * Z)
        self.sems = 384
        self.chunk = B // 2
        self.chunks = 2
        bits = list(range(B.bit_length() - 1))
        self.order_a = tuple(bits[1:] + bits[:1])
        self.order_b = tuple(bits[1:][::-1] + bits[:1])

    def fits(self):
        if self.B & (self.B - 1) or self.B < 4 or self.rd % 8 or self.rf % 8 or self.T % 16 or self.Fb % 128:
            return False
        held = sum(int(np.prod(s.shape)) * jnp.dtype(s.dtype).itemsize for s in scratch_of(self)[3:])
        return held + 12 * self.LK * self.Tq < 67043328


def layer_kernel(p, *refs):
    refs = list(refs)
    take = lambda n: [refs.pop(0) for _ in range(n)]
    len_ref, x, cot, wq, wk, wv, wo, wu, wd, small = take(10)
    out, gin, gqkv, go_ref, gu, gd, gs = take(7)
    send, recv, lsem = take(3)
    x_all, wsend, wz, small_all, vec = take(5)
    qs, kv, lse, osc, asend, arecv, amat = take(7)
    wout, wupz, wup, wdn = take(4)
    hn_all, df_all, yp, dhp, yslot, dhslot = take(6)
    xh1, act, gpr, du = take(4)
    gout, gupz, gup, gdn, gupslot, gdnslot, gurecv, gdn_sum, gz_sum = take(9)
    goutbit, goutline = take(2)
    das, dkv, dqs, dqkv, dxp, dxr, gz = take(7)
    dkslot, gzslot, sslot, zslot, dh0, mixed_t, delta, dq_t = take(8)
    L = Links(p.B, p.Z, send, recv)
    b, z, B, Z = L.b, L.z, p.B, p.Z
    S, T, Tq, Dh, D, Fb = p.S, p.T, p.Tq, p.Dh, p.D, p.Fb
    me = b * Z + z
    nb = B.bit_length() - 1
    cut = 2 * Dh
    half = D // 2

    barrier = pltpu.get_barrier_semaphore()
    for k in range(1, Z):
        pl.semaphore_signal(barrier, inc=1, device_id=(b, lax.rem(z + k, Z)), device_id_type=MESH)
    for k in range(1, B):
        pl.semaphore_signal(barrier, inc=1, device_id=(b ^ k, z), device_id_type=MESH)

    for zi in range(Z):
        cols = slice(zi * Dh, (zi + 1) * Dh)
        wsend[zi] = jnp.concatenate(
            [wk[:, cols], wv[:, cols], wq[:, cols], jnp.zeros((p.rd, p.wide - 3 * Dh), bf16)], axis=1
        )
    pl.semaphore_wait(barrier, Z - 1 + B - 1)

    def block(ref, i, rows):
        return ref.at[pl.ds(pl.multiple_of(i * rows, 8), rows)]

    def column_block(ref, i, rows, first, cols):
        return ref.at[pl.ds(pl.multiple_of(i * rows, 8), rows), pl.ds(first, cols)]

    def hidden_cols(i):
        return pl.ds(pl.multiple_of(i * Fb, 128), Fb)


    jobs = {}

    def go(*names):
        for name in names:
            next(jobs[name], None)

    def finish(*names):
        for name in names:
            for _ in jobs[name]:
                pass

    zbits = tuple(range(Z.bit_length() - 1))[::-1]
    jobs["small_z"] = line_swap(L, lambda zt: small, lambda zi: small_all.at[b, zi])
    jobs["w_z"] = line_swap(L, lambda zt: wsend.at[zt], lambda zi: block(wz, b * Z + zi, p.rd))
    jobs["x"] = line_gather(L, lambda zi: block(x_all, zi, p.rows), own=x)
    jobs["up_b"] = blk_swap(L, lambda bt: wu.at[:, hidden_cols(bt)], lambda bs: wupz.at[z, bs])
    go("small_z", "w_z", "x", "up_b")
    own_copies = [
        pltpu.make_async_copy(x, block(x_all, z, p.rows), lsem.at[0]),
        pltpu.make_async_copy(small, small_all.at[b, z], lsem.at[1]),
        pltpu.make_async_copy(wsend.at[z], block(wz, me, p.rd), lsem.at[2]),
        pltpu.make_async_copy(wo, block(wout, me, p.rd), lsem.at[3]),
        pltpu.make_async_copy(wu.at[:, hidden_cols(b)], wupz.at[z, b], lsem.at[4]),
        pltpu.make_async_copy(wd, wdn.at[z], lsem.at[5]),
    ]
    for c in own_copies:
        c.start()
    for c in own_copies:
        c.wait()
    jobs["small"] = bit_gather(L, lambda i: small_all.at[i], p.order_a)
    jobs["w"] = bit_gather(L, lambda i: column_block(wz, i, Z * p.rd, 0, cut), p.order_a)
    jobs["q"] = bit_gather(L, lambda i: column_block(wz, i, Z * p.rd, cut, p.wide - cut), p.order_b)
    go("small_z", "small", "small", "small", "small", "w_z", "w", "q", "w", "w", "x", "q", "q")
    turns = B - 1
    go(*["small"] * (turns - 3), *["w"] * (turns - 2), *["q"] * (turns - 2), "up_b")

    vec[...] = jnp.concatenate(
        [small_all[i // Z, i % Z][:, : p.rd].astype(f32) for i in range(B * Z)], axis=1
    )
    bias_up = jnp.concatenate([small_all[b, zi][8:9, : p.rf].astype(f32) for zi in range(Z)], axis=1)
    bias_q = jnp.zeros((1, Dh), f32)
    bias_v = jnp.zeros((1, Dh), f32)
    for zi in range(Z):
        bias_q = jnp.where(z == zi, vec[0:1, zi * Dh : (zi + 1) * Dh], bias_q)
        bias_v = jnp.where(z == zi, vec[1:2, zi * Dh : (zi + 1) * Dh], bias_v)
    bias = jnp.concatenate(
        [jnp.zeros((1, Dh), f32), bias_v, bias_q, jnp.zeros((1, p.wide - 3 * Dh), f32)], axis=1
    )

    def project(zi, order, guard):
        def work():
            made = dot(x_all[pl.ds(pl.multiple_of(zi * p.rows, p.rows), p.rows)], wz[...], 1, 0) + bias
            made = made.astype(bf16)
            for s in range(S):
                kv[b, s, zi] = made[s * T : (s + 1) * T, :cut]
                qs[s, zi] = made[s * T : (s + 1) * T, cut:]

        if guard is None:
            work()
        else:
            pl.when(guard)(work)
        yield from bit_gather(L, lambda i: kv.at[i, :, zi], order, guard=guard)

    jobs["c0"] = project(z, p.order_a, None)
    for dist in range(1, Z):
        for way, tag in ((1, "u"), (-1, "d")):
            guard = z >= dist if way > 0 else z + dist < Z
            order = p.order_b if dist % 2 else p.order_a
            jobs[f"c{dist}{tag}"] = project(z - way * dist, order, guard)
    go("c1d", "c0", "c1u")
    for dist in range(2, Z):
        go("x")
        if dist == Z - 1:
            jobs["out_z"] = line_swap(L, lambda zt: wo, lambda zi: block(wout, b * Z + zi, p.rd))
            jobs["up_z"] = bit_gather(L, lambda i: wupz.at[i], zbits, axis="head")
            go("out_z", "up_z")
        go(f"c{dist}d", f"c{dist}u")
        if dist == 2:
            go("c1d", "c1d", "c0", "c0")
        if dist == 3:
            go("c1u", "c1u")
        if dist > 3:
            go(f"c{dist - 2}u", f"c{dist - 2}d", f"c{dist - 2}u", f"c{dist - 2}d")
    for dist in range(max(Z - 2, 2), Z):
        go(*[f"c{dist}{tag}" for tag in "dduu"])
    parts = ["c0"] + [f"c{dist}{tag}" for dist in range(1, Z) for tag in "du"]
    go(*parts, "up_z", "out_z")
    jobs["out"] = bit_gather(L, lambda i: block(wout, i, Z * p.rd), p.order_a)
    go("out")
    for name in parts:
        for _ in jobs[name]:
            pass

    key_at = lax.broadcasted_iota(jnp.int32, (p.LK, Tq), 0)

    def head_cols(h, part):
        return slice(part * Dh + h * HEAD_DIM, part * Dh + (h + 1) * HEAD_DIM)

    def attend(s):
        parts = []
        for h in range(p.heads):
            k_h = kv[:, s, :, :, head_cols(h, 0)].reshape(p.LK, HEAD_DIM)
            v_h = kv[:, s, :, :, head_cols(h, 1)].reshape(p.LK, HEAD_DIM)
            q_h = qs[s, :, :, h * HEAD_DIM : (h + 1) * HEAD_DIM].reshape(Tq, HEAD_DIM)
            scores = dot(k_h, q_h, 1, 1) * HEAD_DIM ** (-0.5)
            scores = jnp.where(key_at < len_ref[s], scores, neg_big)
            top = jnp.max(scores, axis=0, keepdims=True)
            weights = jnp.exp(scores - top)
            total = jnp.sum(weights, axis=0, keepdims=True)
            mixed = dot(v_h, weights.astype(bf16), 0, 0) / total
            lse[s * p.heads + h] = top + jnp.log(total)
            mixed_t[s * p.heads + h] = mixed
            parts.append(mixed.T)
        osc[s] = jnp.concatenate(parts, axis=1).astype(bf16)

    for s in range(S):
        attend(s)
        go("out", "out", "out", "up_z")

    for zi in range(Z):
        asend[zi] = jnp.concatenate([osc[s, zi * T : (zi + 1) * T] for s in range(S)], axis=1)
    swap_a = line_swap(L, lambda zt: asend.at[zt], lambda zi: arecv.at[zi])
    next(swap_a)
    arecv[z] = asend[z]
    jobs["down_z"] = bit_gather(L, lambda i: wdn.at[i], zbits, axis="head")
    go("down_z")
    go(*["out"] * turns)
    next(swap_a)
    for s in range(S):
        amat[s * T : (s + 1) * T] = jnp.concatenate(
            [arecv[zi][:, s * Dh : (s + 1) * Dh] for zi in range(Z)], axis=1
        )

    h0 = x[...].astype(f32) + dot(amat[...], wout[...], 1, 0) + vec[2:3]
    unit, scale1 = normed(h0)
    xh1[...] = unit
    hn = (unit * vec[3:4] + vec[4:5]).astype(bf16)
    hn_all[b] = hn

    def row_gather(ref):
        jobs = [
            bit_gather(L, lambda i: ref.at[i, :, pl.ds(0, half)], p.order_a),
            bit_gather(L, lambda i: ref.at[i, :, pl.ds(half, half)], p.order_b),
        ]
        pump(jobs)
        return jobs

    def row_reduce(ref, slot):
        step = lambda d, r: add_rows(d, r, p.rows)
        jobs = [
            bit_reduce(
                L, lambda i: ref.at[i, :, pl.ds(0, half)], lambda m: slot.at[m - 1, :, pl.ds(0, half)], p.order_a, step
            ),
            bit_reduce(
                L, lambda i: ref.at[i, :, pl.ds(half, half)], lambda m: slot.at[m - 1, :, pl.ds(half, half)],
                p.order_b, step,
            ),
        ]
        pump(jobs)
        return jobs

    h_jobs = row_gather(hn_all)
    go("down_z")
    finish("up_z")
    for i in range(B * Z):
        wup[i * p.rd : (i + 1) * p.rd] = wupz[i % Z, i // Z]
    drain(h_jobs)
    finish("down_z")

    pair = 2
    wide_rows = pair * p.rows

    def up_down(c, carry):
        at = pl.ds(pl.multiple_of(c * wide_rows, wide_rows), wide_rows)
        rows_in = hn_all[pl.ds(c * pair, pair)].reshape(wide_rows, D)
        u = dot(rows_in, wup[...], 1, 0) + bias_up
        e = 1.0 + lax.erf(u * np.float32(np.sqrt(0.5)))
        g = (0.5 * u * e).astype(bf16)
        act[at] = g
        gpr[at] = 0.5 * e + u * jnp.exp(-0.5 * u * u) * np.float32(1 / np.sqrt(2 * np.pi))
        yp[pl.ds(c * pair, pair)] = dot(g, wdn[...].reshape(Fb, D), 1, 0).astype(bf16).reshape(pair, p.rows, D)
        return carry

    lax.fori_loop(0, B // pair, up_down, 0)
    drain(row_reduce(yp, yslot))

    y0 = hn.astype(f32) + yp[b].astype(f32) + vec[5:6]
    unit2, scale2 = normed(y0)
    out[...] = (unit2 * vec[6:7] + vec[7:8]).astype(bf16)
    place = me * T + lax.broadcasted_iota(jnp.int32, (T, D), 0)
    dy = jnp.concatenate(
        [jnp.where(place < len_ref[s], cot[s * T : (s + 1) * T].astype(f32), 0.0) for s in range(S)], axis=0
    )
    column = lambda v: jnp.sum(v, axis=0, keepdims=True)
    dy0 = norm_back(dy, vec[6:7], unit2, scale2)
    df = dy0.astype(bf16)
    df_all[b] = df
    f_jobs = row_gather(df_all)
    gs_rows = {5: column(df.astype(f32)), 6: column(dy * unit2), 7: column(dy)}
    drain(f_jobs)

    def back(c, carry):
        at = pl.ds(pl.multiple_of(c * wide_rows, wide_rows), wide_rows)
        dg = dot(df_all[pl.ds(c * pair, pair)].reshape(wide_rows, D), wdn[...].reshape(Fb, D), 1, 1)
        d = (gpr[at] * dg).astype(bf16)
        du[at] = d
        dhp[pl.ds(c * pair, pair)] = dot(d, wup[...], 1, 1).astype(bf16).reshape(pair, p.rows, D)
        return carry + column(d.astype(f32))

    grad_up = lax.fori_loop(0, B // pair, back, jnp.zeros((1, Fb), f32))
    jobs["h0"], jobs["h1"] = row_reduce(dhp, dhslot)
    gdn_sum[...] = jnp.zeros((Fb, D), f32)

    def down_terms(c, carry):
        at = pl.ds(pl.multiple_of(c * wide_rows, wide_rows), wide_rows)
        gdn_sum[...] += dot(act[at], df_all[pl.ds(c * pair, pair)].reshape(wide_rows, D), 0, 0)
        return carry

    lax.fori_loop(0, B // pair, down_terms, 0)
    for zi in range(Z):
        gdn[zi] = gdn_sum[zi * p.rf : (zi + 1) * p.rf].astype(bf16)
    jobs["gd"] = bit_reduce(
        L, lambda i: gdn.at[i], lambda m: gdnslot.at[m - 1], zbits, lambda d, r: add_rows(d, r, p.rf), axis="head"
    )
    first = B // 2
    go("gd", *["h0"] * first, *["h1"] * first)
    gup[...] = jnp.zeros((D, Fb), f32)

    def up_terms(c, carry):
        at = pl.ds(pl.multiple_of(c * wide_rows, wide_rows), wide_rows)
        gup[...] += dot(hn_all[pl.ds(c * pair, pair)].reshape(wide_rows, D), du[at], 0, 0)
        return carry

    lax.fori_loop(0, B // pair, up_terms, 0)
    for i in range(B * Z):
        gupz[i % Z, i // Z] = gup[i * p.rd : (i + 1) * p.rd].astype(bf16)
    go(*["h0", "h1"] * first)
    dh = dy0 + dhp[b].astype(f32)
    gs_rows[3], gs_rows[4] = column(dh * xh1[...]), column(dh)
    grad_h0 = norm_back(dh, vec[3:4], xh1[...], scale1)
    dh0[...] = grad_h0
    db = grad_h0.astype(bf16)
    gs_rows[2] = column(db.astype(f32))
    da = dot(db, wout[...], 1, 1).astype(bf16)
    for _ in swap_a:
        pass
    for zi in range(Z):
        asend[zi] = jnp.concatenate(
            [da[s * T : (s + 1) * T, zi * Dh : (zi + 1) * Dh] for s in range(S)], axis=1
        )
    swap_d = line_swap(L, lambda zt: asend.at[zt], lambda zi: das.at[zi])
    next(swap_d)
    das[z] = asend[z]

    def add_gup(d, r):
        for i in range(B):
            d[i] = (d[i].astype(f32) + r[i].astype(f32)).astype(bf16)

    jobs["gu"] = bit_reduce(
        L, lambda i: gupz.at[i], lambda m: gupslot.at[m - 1], zbits, add_gup, axis="head"
    )
    go("gd", "gd", "gu")
    gout[...] = dot(amat[...], db, 0, 0).astype(bf16)
    jobs["go"] = bit_reduce(
        L, lambda i: block(gout, i, Z * p.rd), lambda m: goutbit.at[m - 1], p.order_a,
        lambda d, r: add_rows(d, r, p.rd),
    )
    go("go")
    next(swap_d)
    for s in range(S):
        osc[s] = jnp.concatenate([das[zi][:, s * Dh : (s + 1) * Dh] for zi in range(Z)], axis=0)

    for s in range(S):
        for h in range(p.heads):
            da_t = osc[s, :, h * HEAD_DIM : (h + 1) * HEAD_DIM].astype(f32).T
            delta[s * p.heads + h] = column(da_t * mixed_t[s * p.heads + h])
    dq_t[...] = jnp.zeros(dq_t.shape, f32)
    part = p.chunk * Tq
    key_in = lax.broadcasted_iota(jnp.int32, (part, Tq), 0)

    def attend_back(turn, carry):
        s, c = turn // p.chunks, turn % p.chunks
        blocks = pl.ds(c * p.chunk, p.chunk)
        keys, vals, sums = [], [], []
        for h in range(p.heads):
            k_h = kv[blocks, s, :, :, head_cols(h, 0)].reshape(part, HEAD_DIM)
            v_h = kv[blocks, s, :, :, head_cols(h, 1)].reshape(part, HEAD_DIM)
            q_h = qs[s, :, :, h * HEAD_DIM : (h + 1) * HEAD_DIM].reshape(Tq, HEAD_DIM)
            da_h = osc[s][:, h * HEAD_DIM : (h + 1) * HEAD_DIM]
            scores = dot(k_h, q_h, 1, 1) * HEAD_DIM ** (-0.5)
            probs = jnp.exp(scores - lse[s * p.heads + h])
            probs = jnp.where(key_in < len_ref[s] - c * part, probs, 0.0)
            terms = dot(probs.astype(bf16), da_h, 1, 0)
            sums.append(column(terms))
            vals.append(terms.astype(bf16))
            gp = dot(v_h, da_h, 1, 1)
            ds = (probs * (gp - delta[s * p.heads + h])).astype(bf16)
            keys.append((dot(ds, q_h, 1, 0) * HEAD_DIM ** (-0.5)).astype(bf16))
            dq_t[s * p.heads + h] += dot(k_h, ds, 0, 0)
        dkv[blocks, s] = jnp.concatenate(keys + vals, axis=1).reshape(p.chunk, Z, T, cut)
        return carry + jnp.concatenate(sums, axis=1)

    sums_v = lax.fori_loop(0, S * p.chunks, attend_back, jnp.zeros((1, Dh), f32))
    for s in range(S):
        dqs[s] = jnp.concatenate(
            [(dq_t[s * p.heads + h] * HEAD_DIM ** (-0.5)).T.astype(bf16) for h in range(p.heads)], axis=1
        ).reshape(Z, T, Dh)

    sum_q, sum_v = jnp.zeros((1, Dh), f32), sums_v
    for s in range(S):
        sum_q = sum_q + column(dqs[s].reshape(Tq, Dh).astype(f32))
    zero = jnp.zeros((1, Dh), f32)
    for row, mine in ((0, sum_q), (1, sum_v)):
        gs_rows[row] = jnp.concatenate([jnp.where(z == zi, mine, zero) for zi in range(Z)], axis=1)
    spread = jnp.concatenate([jnp.where(b == i, grad_up, 0.0) for i in range(B)], axis=1)
    for j in range(4):
        gs_rows[8 + j] = spread[:, j * D : (j + 1) * D]
    gs[...] = jnp.concatenate([gs_rows[i] for i in range(12)] + [jnp.zeros((4, D), f32)], axis=0)

    def small_sums():
        base = L.take(nb)
        for bit in range(nb):
            c = L.copy(gs, sslot.at[bit], base + bit, b ^ (1 << bit), z)
            c.start()
            yield
            c.wait()
            gs[...] += sslot[bit]
        swap = line_swap(L, lambda zt: gs, lambda zi: zslot.at[zi])
        next(swap)
        zslot[z] = gs[...]
        yield
        for _ in swap:
            pass
        total = zslot[0]
        for zi in range(1, Z):
            total = total + zslot[zi]
        gs[...] = total

    jobs["sum"] = small_sums()
    go("sum")

    def add_kv(d, r):
        for s in range(S):
            d[s] = (d[s].astype(f32) + r[s].astype(f32)).astype(bf16)

    pad = jnp.zeros((T, p.wide - 3 * Dh), bf16)
    dx_base = L.take(Z)
    gz_sum[...] = jnp.zeros((D, p.wide), f32)

    def dx_copy(src, zi, zs):
        return L.copy(block(dxp, src, p.rows), dxr.at[zs], dx_base + lax.rem(zi - zs + Z, Z), b, zi)

    def project_back(zi):
        for s in range(S):
            at = slice(zi * p.rows + s * T, zi * p.rows + (s + 1) * T)
            dqkv[at] = jnp.concatenate([dkv[b, s, zi], dqs[s, zi], pad], axis=1)
        at = slice(zi * p.rows, (zi + 1) * p.rows)
        dxp[at] = dot(dqkv[at], wz[...], 1, 1).astype(bf16)
        pl.when(z != zi)(lambda: dx_copy(zi, zi, z).start())

    def weight_terms(zi):
        at = slice(zi * p.rows, (zi + 1) * p.rows)
        gz_sum[...] += dot(x_all[at], dqkv[at], 0, 0)

    turn_z = []
    for j in range((Z + 1) // 2):
        turn_z += [Z - 1 - j] + ([j] if j < Z - 1 - j else [])
    for n, zi in enumerate(turn_z):
        jobs[f"d{n}"] = bit_reduce(
            L, lambda i, zi=zi: dkv.at[i, :, zi], lambda m, zi=zi: dkslot.at[zi, m - 1],
            p.order_b if n % 2 else p.order_a, add_kv,
        )
        go(f"d{n}")
    go("gu", "gu", *["go"] * first)
    rest = turns - first
    for n in range(0, Z, 2):
        go(*[f"d{n}"] * first, "sum", *[f"d{n + 1}"] * first)
        for _ in range(rest - 1):
            go(f"d{n}", f"d{n + 1}")
        if n + 2 >= Z:
            go("gu", "gd", *["go"] * rest)
            for k in range(n):
                weight_terms(turn_z[k])
        for k in (n, n + 1):
            go(f"d{k}")
            project_back(turn_z[k])
        if n + 2 < Z:
            go("sum")
    for k in (Z - 2, Z - 1):
        weight_terms(turn_z[k])
    gz[...] = gz_sum[...].astype(bf16)
    step = lambda d, r: add_rows(d, r, p.rd)
    jobs["gz0"] = bit_reduce(
        L, lambda i: column_block(gz, i, Z * p.rd, 0, cut), lambda m: gzslot.at[m - 1, :, pl.ds(0, cut)], p.order_a, step
    )
    jobs["gz1"] = bit_reduce(
        L, lambda i: column_block(gz, i, Z * p.rd, cut, p.wide - cut),
        lambda m: gzslot.at[m - 1, :, pl.ds(cut, p.wide - cut)], p.order_b, step,
    )
    go("gz0", "gz1")
    finish("gu", "gd", "go")
    jobs["gu_b"] = blk_swap(L, lambda bt: gupz.at[z, bt], lambda bs: gurecv.at[bs])
    jobs["go_z"] = line_swap(L, lambda zt: block(gout, b * Z + zt, p.rd), lambda zi: goutline.at[zi])
    go(*["gz0"] * first, *["gz1"] * first, *["gz0", "gz1"] * rest)
    jobs["gz_z"] = line_swap(L, lambda zt: block(gz, b * Z + zt, p.rd), lambda zi: gqkv.at[zi])
    go("gz_z", "gu_b", "go_z")
    gqkv[z] = gz[pl.ds(pl.multiple_of(me * p.rd, 8), p.rd)]
    gurecv[b] = gupz[z, b]
    goutline[z] = gout[pl.ds(pl.multiple_of(me * p.rd, 8), p.rd)]
    dxr[z] = dxp[pl.ds(pl.multiple_of(z * p.rows, 8), p.rows)]
    gd[...] = gdn[z].astype(f32)
    for zi in range(Z):
        pl.when(z != zi)(lambda zi=zi: dx_copy(zi, z, zi).wait_recv())
    sum_of = lambda ref: functools.reduce(lambda u, v: u + v, [ref[zi].astype(f32) for zi in range(Z)])
    gin[...] = dh0[...] + sum_of(dxr)
    for job in jobs.values():
        for _ in job:
            pass
    go_sum = sum_of(goutline)
    go_ref[...] = go_sum
    gu[...] = jnp.concatenate([gurecv[i].astype(f32) for i in range(B)], axis=1)
    for zi in range(Z):
        pl.when(z != zi)(lambda zi=zi: dx_copy(zi, zi, z).wait_send())
    for job in (swap_a, swap_d):
        for _ in job:
            pass
    assert L.used <= send.shape[0], L.used


def scratch_of(p):
    B, Z, S, T, Tq, D, F, Dh, Fb = p.B, p.Z, p.S, p.T, p.Tq, p.D, p.F, p.Dh, p.Fb
    V = pltpu.VMEM
    cut = 2 * Dh
    heads = S * p.heads
    return [
        pltpu.SemaphoreType.DMA((p.sems,)),
        pltpu.SemaphoreType.DMA((p.sems,)),
        pltpu.SemaphoreType.DMA((6,)),
        V((p.R, D), bf16), V((Z, p.rd, p.wide), bf16), V((D, p.wide), bf16), V((B, Z, 16, 128), bf16), V((16, D), f32),
        V((S, Z, T, p.wide - cut), bf16), V((B, S, Z, T, cut), bf16), V((heads, 1, Tq), f32),
        V((S, Tq, Dh), bf16), V((Z, T, S * Dh), bf16), V((Z, T, S * Dh), bf16), V((p.rows, D), bf16),
        V((D, D), bf16), V((Z, B, p.rd, Fb), bf16), V((D, Fb), bf16), V((Z, p.rf, D), bf16),
        V((B, p.rows, D), bf16), V((B, p.rows, D), bf16), V((B, p.rows, D), bf16), V((B, p.rows, D), bf16),
        V((B - 1, p.rows, D), bf16), V((B - 1, p.rows, D), bf16),
        V((p.rows, D), f32), V((B * p.rows, Fb), bf16), V((B * p.rows, Fb), f32), V((B * p.rows, Fb), bf16),
        V((D, D), bf16), V((Z, B, p.rd, Fb), bf16), V((D, Fb), f32), V((Z, p.rf, D), bf16), V((Z - 1, B, p.rd, Fb), bf16),
        V((Z - 1, p.rf, D), bf16), V((B, p.rd, Fb), bf16), V((Fb, D), f32), V((D, p.wide), f32),
        V((B - 1, Z * p.rd, D), bf16), V((Z, p.rd, D), bf16),
        V((Z, T, S * Dh), bf16), V((B, S, Z, T, cut), bf16), V((S, Z, T, Dh), bf16), V((p.R, p.wide), bf16),
        V((p.R, D), bf16), V((Z, p.rows, D), bf16), V((D, p.wide), bf16),
        V((Z, B - 1, S, T, cut), bf16), V((B - 1, Z * p.rd, p.wide), bf16), V((B.bit_length(), 16, D), f32),
        V((Z, 16, D), f32), V((p.rows, D), f32), V((heads, HEAD_DIM, Tq), f32), V((heads, 1, Tq), f32),
        V((heads, HEAD_DIM, Tq), f32),
    ]


def spread_kernel(p, *refs):
    ins, outs = refs[:7], refs[7:]
    out, gin, gqkv, go, gu, gd, gs = ins
    outs[0][...] = out[...]
    outs[1][...] = gin[...]
    for n, at in ((2, 2), (4, 0), (5, 1)):
        outs[n][...] = jnp.concatenate(
            [gqkv[zi][:, at * p.Dh : (at + 1) * p.Dh].astype(f32) for zi in range(p.Z)], axis=1
        )
    outs[7][...] = go[...]
    outs[11][...] = gu[...]
    outs[13][...] = gd[...]
    me = lax.axis_index("blk") * p.Z + lax.axis_index("head")
    mine = pltpu.roll(gs[...], lax.rem(p.D - me * p.rd, p.D), 1)
    for n, row in ((3, 0), (6, 1), (8, 2), (9, 3), (10, 4), (14, 5), (15, 6), (16, 7)):
        outs[n][...] = mine[row : row + 1, : p.rd]
    each = p.D // p.rf
    row_u = jnp.zeros((8, p.D), f32)
    for j in range(p.F // p.D):
        row_u = jnp.where(me // each == j, jnp.broadcast_to(gs[8 + j : 9 + j], (8, p.D)), row_u)
    outs[12][...] = pltpu.roll(row_u, lax.rem(p.D - (me % each) * p.rf, p.D), 1)[0:1, : p.rf]


def layer(p, hidden_in, cotangent, lengths, weights):
    (w_query, b_query, w_key, w_value, b_value, w_out, b_out, gain_one, shift_one, w_up, b_up, w_down, b_down,
     gain_two, shift_two) = weights
    D, F, Z = p.D, p.F, p.Z
    rows = [b_query, b_value, b_out, gain_one, shift_one, b_down, gain_two, shift_two, b_up]
    gap = lambda v: jnp.zeros((128 - v.shape[0],), bf16)
    small = jnp.concatenate([piece for v in rows for piece in (v, gap(v))] + [jnp.zeros(((16 - len(rows)) * 128,), bf16)])
    small = small.reshape(16, 128)
    vmem = pl.BlockSpec(memory_space=pltpu.VMEM)
    shape = jax.ShapeDtypeStruct
    results = pl.pallas_call(
        functools.partial(layer_kernel, p),
        out_shape=[
            shape((p.rows, D), bf16), shape((p.rows, D), f32), shape((Z, p.rd, p.wide), bf16),
            shape((p.rd, D), f32), shape((p.rd, F), f32), shape((p.rf, D), f32), shape((16, D), f32),
        ],
        in_specs=[pl.BlockSpec(memory_space=pltpu.SMEM)] + [vmem] * 9,
        out_specs=[vmem] * 7,
        scratch_shapes=scratch_of(p),
        compiler_params=pltpu.CompilerParams(
            collective_id=0, has_side_effects=True, vmem_limit_bytes=67043328
        ),
        name="layer",
    )(
        lengths, hidden_in.reshape(p.rows, D), cotangent.reshape(p.rows, D), w_query, w_key, w_value, w_out, w_up,
        w_down, small,
    )
    wide, square = shape((p.rows, D), f32), shape((p.rd, D), f32)
    vector = shape((1, p.rd), f32)
    flat = pl.pallas_call(
        functools.partial(spread_kernel, p),
        out_shape=[
            shape((p.rows, D), bf16), wide, square, vector, square, square, vector, square, vector, vector, vector,
            shape((p.rd, F), f32), shape((1, p.rf), f32), shape((p.rf, D), f32), vector, vector, vector,
        ],
        in_specs=[vmem] * 7,
        out_specs=[vmem] * 17,
        name="spread",
    )(*results)
    shape3 = (p.S, p.T, D)
    return tuple(
        v.reshape(shape3) if n < 2 else v.reshape(-1) if v.shape[0] == 1 else v for n, v in enumerate(flat)
    )


def passed_along(value, axis, steps):
    count = lax.axis_size(axis)
    pairs = [(source, (source + steps) % count) for source in range(count)]
    return lax.ppermute(value, axis, pairs)


def layer_norm(entries, norm_gain, norm_shift):
    average = jnp.mean(entries, axis=-1, keepdims=True)
    centred = entries - average
    spread = jnp.mean(centred * centred, axis=-1, keepdims=True)
    return centred * lax.rsqrt(spread + norm_eps) * norm_gain + norm_shift


def gelu_exact(values_in):
    return jax.nn.gelu(values_in, approximate=False)


def key_valid(lengths, start, rows_here):
    positions = start + jnp.arange(rows_here, dtype=jnp.int32)
    return positions[None, :] < lengths[:, None]


def scores_of(query_four, key_four, valid):
    raw_scores = jnp.einsum(
        "sqhd,skhd->shqk", query_four, key_four, preferred_element_type=jnp.float32
    ) * HEAD_DIM ** (-0.5)
    return jnp.where(valid[:, None, None, :], raw_scores, neg_big)


def sweep(step_fn, carry, key_piece, value_piece, width):
    blocks_in = key_piece.shape[1] // width

    def one_block(which_block, running):
        begin = which_block * width
        key_part = lax.dynamic_slice_in_dim(key_piece, begin, width, 1)
        value_part = lax.dynamic_slice_in_dim(value_piece, begin, width, 1)
        return step_fn(running, key_part, value_part, begin)

    return lax.fori_loop(0, blocks_in, one_block, carry)


def plain_body(
    hidden_in,
    cotangent,
    lengths,
    w_query,
    b_query,
    w_key,
    w_value,
    b_value,
    w_out,
    b_out,
    gain_one,
    shift_one,
    w_up,
    b_up,
    w_down,
    b_down,
    gain_two,
    shift_two,
):
    gathered = (
        lax.all_gather(w_query, ("blk", "head"), axis=0, tiled=True),
        lax.all_gather(b_query, ("blk", "head"), axis=0, tiled=True),
        lax.all_gather(w_key, ("blk", "head"), axis=0, tiled=True),
        lax.all_gather(w_value, ("blk", "head"), axis=0, tiled=True),
        lax.all_gather(b_value, ("blk", "head"), axis=0, tiled=True),
        lax.all_gather(w_out, ("blk", "head"), axis=0, tiled=True),
        lax.all_gather(b_out, ("blk", "head"), axis=0, tiled=True),
        lax.all_gather(gain_one, ("blk", "head"), axis=0, tiled=True),
        lax.all_gather(shift_one, ("blk", "head"), axis=0, tiled=True),
        lax.all_gather(w_up, ("blk", "head"), axis=0, tiled=True),
        lax.all_gather(b_up, ("blk", "head"), axis=0, tiled=True),
        lax.all_gather(w_down, ("blk", "head"), axis=0, tiled=True),
        lax.all_gather(b_down, ("blk", "head"), axis=0, tiled=True),
        lax.all_gather(gain_two, ("blk", "head"), axis=0, tiled=True),
        lax.all_gather(shift_two, ("blk", "head"), axis=0, tiled=True),
    )
    query_mat, query_bias, key_mat, value_mat, value_bias, out_mat, out_bias = gathered[0:7]
    gain_first, shift_first, up_mat, up_bias, down_mat, down_bias, gain_second, shift_second = (
        gathered[7:15]
    )
    seqs, tokens, width = hidden_in.shape
    rows = hidden_in.reshape(seqs * tokens, width)
    queries = (
        jnp.dot(rows, query_mat, preferred_element_type=f32) + query_bias.astype(f32)
    ).astype(bf16)
    keys = jnp.dot(rows, key_mat, preferred_element_type=f32).astype(bf16)
    values = (jnp.dot(rows, value_mat, preferred_element_type=f32) + value_bias.astype(f32)).astype(
        bf16
    )
    queries_h, keys_h, values_h = (
        lax.all_to_all(
            queries.reshape(seqs, tokens, width), "head", split_axis=2, concat_axis=1, tiled=True
        ),
        lax.all_to_all(
            keys.reshape(seqs, tokens, width), "head", split_axis=2, concat_axis=1, tiled=True
        ),
        lax.all_to_all(
            values.reshape(seqs, tokens, width), "head", split_axis=2, concat_axis=1, tiled=True
        ),
    )
    head_groups = lax.axis_size("head")
    group_rows = tokens * head_groups
    local_width = width // head_groups
    heads_here = local_width // HEAD_DIM
    query_four = queries_h.reshape(seqs, group_rows, heads_here, HEAD_DIM)
    cycle_size = lax.axis_size("blk")
    cycle_index = lax.axis_index("blk")

    def forward_step(carry, key_part, value_part, start):
        run_max, run_total, accum = carry
        rows_here = key_part.shape[1]
        key_four = key_part.reshape(seqs, rows_here, heads_here, HEAD_DIM)
        value_four = value_part.reshape(seqs, rows_here, heads_here, HEAD_DIM)
        valid = key_valid(lengths, start, rows_here)
        scores = scores_of(query_four, key_four, valid)
        new_max = jnp.maximum(run_max, jnp.max(scores, axis=-1))
        weights = jnp.where(valid[:, None, None, :], jnp.exp(scores - new_max[..., None]), 0.0)
        factor = jnp.exp(run_max - new_max)
        run_total = run_total * factor + jnp.sum(weights, axis=-1)
        accum = accum * factor[..., None] + jnp.einsum(
            "shqk,skhd->shqd", weights.astype(bf16), value_four, preferred_element_type=f32
        )
        return (new_max, run_total, accum)

    initial = (
        jnp.full((seqs, heads_here, group_rows), neg_big, f32),
        jnp.zeros((seqs, heads_here, group_rows), f32),
        jnp.zeros((seqs, heads_here, group_rows, HEAD_DIM), f32),
    )
    run_max, run_total, accum = sweep(
        forward_step,
        initial,
        lax.all_gather(keys_h, "blk", axis=1, tiled=True),
        lax.all_gather(values_h, "blk", axis=1, tiled=True),
        group_rows,
    )
    attn_out = accum / run_total[..., None]
    log_total = run_max + jnp.log(run_total)
    mixed_h = (
        jnp.transpose(attn_out, (0, 2, 1, 3)).reshape(seqs, group_rows, local_width).astype(bf16)
    )
    mixed = lax.all_to_all(mixed_h, "head", split_axis=1, concat_axis=2, tiled=True).reshape(
        seqs * tokens, width
    )
    branch = jnp.dot(mixed, out_mat, preferred_element_type=f32) + out_bias.astype(f32)
    first_sum = rows.astype(f32) + branch
    normed, norm_back_one = jax.vjp(
        layer_norm, first_sum, gain_first.astype(f32), shift_first.astype(f32)
    )
    normed_low = normed.astype(bf16)
    up_pre = jnp.dot(normed_low, up_mat, preferred_element_type=f32) + up_bias.astype(f32)
    activated, gelu_back = jax.vjp(gelu_exact, up_pre)
    act_low = activated.astype(bf16)
    second = jnp.dot(act_low, down_mat, preferred_element_type=f32) + down_bias.astype(f32)
    second_sum = normed_low.astype(f32) + second
    result, norm_back_two = jax.vjp(
        layer_norm, second_sum, gain_second.astype(f32), shift_second.astype(f32)
    )
    output = result.astype(bf16).reshape(seqs, tokens, width)
    token_block = cycle_index * head_groups + lax.axis_index("head")
    positions = token_block * tokens + jnp.arange(tokens, dtype=jnp.int32)
    row_valid = (positions[None, :] < lengths[:, None]).astype(f32)
    grad_result = (cotangent.astype(f32) * row_valid[:, :, None]).reshape(seqs * tokens, width)
    grad_second_sum, grad_gain_two, grad_shift_two = norm_back_two(grad_result)
    grad_second = grad_second_sum.astype(bf16)
    grad_down_bias = jnp.sum(grad_second.astype(f32), axis=0)
    grad_down_mat = jnp.einsum("rf,rd->fd", act_low, grad_second, preferred_element_type=f32)
    grad_act = jnp.einsum("rd,fd->rf", grad_second, down_mat, preferred_element_type=f32)
    (grad_up_pre,) = gelu_back(grad_act)
    grad_up_low = grad_up_pre.astype(bf16)
    grad_up_bias = jnp.sum(grad_up_low.astype(f32), axis=0)
    grad_up_mat = jnp.einsum("rd,rf->df", normed_low, grad_up_low, preferred_element_type=f32)
    grad_normed = grad_second_sum + jnp.einsum(
        "rf,df->rd", grad_up_low, up_mat, preferred_element_type=f32
    )
    grad_first_sum, grad_gain_one, grad_shift_one = norm_back_one(grad_normed)
    grad_branch = grad_first_sum.astype(bf16)
    grad_out_bias = jnp.sum(grad_branch.astype(f32), axis=0)
    grad_out_mat = jnp.einsum("rd,re->de", mixed, grad_branch, preferred_element_type=f32)
    grad_mixed = jnp.einsum("re,de->rd", grad_branch, out_mat, preferred_element_type=f32).astype(
        bf16
    )
    grad_heads = lax.all_to_all(
        grad_mixed.reshape(seqs, tokens, width), "head", split_axis=2, concat_axis=1, tiled=True
    )
    grad_four = grad_heads.reshape(seqs, group_rows, heads_here, HEAD_DIM)
    delta = jnp.einsum("shqd,sqhd->shq", attn_out, grad_four.astype(f32))

    def backward_step(query_in, grad_in, lse_in, delta_in, key_part, value_part, start):
        rows_here = key_part.shape[1]
        key_four = key_part.reshape(seqs, rows_here, heads_here, HEAD_DIM)
        value_four = value_part.reshape(seqs, rows_here, heads_here, HEAD_DIM)
        valid = key_valid(lengths, start, rows_here)
        scores = scores_of(query_in, key_four, valid)
        probs = jnp.where(valid[:, None, None, :], jnp.exp(scores - lse_in[..., None]), 0.0)
        grad_probs = jnp.einsum("sqhd,skhd->shqk", grad_in, value_four, preferred_element_type=f32)
        grad_scores = (probs * (grad_probs - delta_in[..., None])).astype(bf16)
        part_query = jnp.einsum(
            "shqk,skhd->sqhd", grad_scores, key_four, preferred_element_type=f32
        ) * HEAD_DIM ** (-0.5)
        part_key = jnp.einsum(
            "shqk,sqhd->skhd", grad_scores, query_in, preferred_element_type=f32
        ) * HEAD_DIM ** (-0.5)
        part_value = jnp.einsum(
            "shqk,sqhd->skhd", probs.astype(bf16), grad_in, preferred_element_type=f32
        )
        return (
            part_query,
            part_key.reshape(seqs, rows_here, local_width),
            part_value.reshape(seqs, rows_here, local_width),
        )

    zero_query = jnp.zeros((seqs, group_rows, heads_here, HEAD_DIM), f32)
    zero_rows = jnp.zeros((seqs, group_rows, local_width), f32)

    def cycle_turn(turn, state):
        key_part, value_part, key_accum, value_accum, query_accum = state
        owner = (cycle_index - turn) % cycle_size
        part_query, part_key, part_value = backward_step(
            query_four, grad_four, log_total, delta, key_part, value_part, owner * group_rows
        )
        moved = passed_along((key_part, value_part), "blk", 1)
        returned = (
            passed_along((key_accum + part_key).astype(jnp.bfloat16), "blk", 1).astype(jnp.float32),
            passed_along((value_accum + part_value).astype(jnp.bfloat16), "blk", 1).astype(
                jnp.float32
            ),
        )
        return (moved[0], moved[1], returned[0], returned[1], query_accum + part_query)

    state = lax.fori_loop(
        0, cycle_size, cycle_turn, (keys_h, values_h, zero_rows, zero_rows, zero_query)
    )
    grad_keys_h = state[2]
    grad_values_h = state[3]
    grad_query_four = state[4]
    grad_query_h = grad_query_four.reshape(seqs, group_rows, local_width)
    sent_back = (
        lax.all_to_all(grad_query_h.astype(bf16), "head", split_axis=1, concat_axis=2, tiled=True),
        lax.all_to_all(grad_keys_h.astype(bf16), "head", split_axis=1, concat_axis=2, tiled=True),
        lax.all_to_all(grad_values_h.astype(bf16), "head", split_axis=1, concat_axis=2, tiled=True),
    )
    grad_q_rows = sent_back[0].reshape(seqs * tokens, width)
    grad_k_rows = sent_back[1].reshape(seqs * tokens, width)
    grad_v_rows = sent_back[2].reshape(seqs * tokens, width)
    grad_query_bias = jnp.sum(grad_q_rows.astype(f32), axis=0)
    grad_value_bias = jnp.sum(grad_v_rows.astype(f32), axis=0)
    grad_query_mat = jnp.einsum("rd,re->de", rows, grad_q_rows, preferred_element_type=f32)
    grad_key_mat = jnp.einsum("rd,re->de", rows, grad_k_rows, preferred_element_type=f32)
    grad_value_mat = jnp.einsum("rd,re->de", rows, grad_v_rows, preferred_element_type=f32)
    grad_rows = grad_first_sum + jnp.einsum(
        "re,de->rd", grad_q_rows, query_mat, preferred_element_type=f32
    )
    grad_rows = grad_rows + jnp.einsum(
        "re,de->rd", grad_k_rows, key_mat, preferred_element_type=f32
    )
    grad_rows = grad_rows + jnp.einsum(
        "re,de->rd", grad_v_rows, value_mat, preferred_element_type=f32
    )
    shards = (
        lax.psum_scatter(grad_query_mat, ("blk", "head"), scatter_dimension=0, tiled=True),
        lax.psum_scatter(grad_query_bias, ("blk", "head"), scatter_dimension=0, tiled=True),
        lax.psum_scatter(grad_key_mat, ("blk", "head"), scatter_dimension=0, tiled=True),
        lax.psum_scatter(grad_value_mat, ("blk", "head"), scatter_dimension=0, tiled=True),
        lax.psum_scatter(grad_value_bias, ("blk", "head"), scatter_dimension=0, tiled=True),
        lax.psum_scatter(grad_out_mat, ("blk", "head"), scatter_dimension=0, tiled=True),
        lax.psum_scatter(grad_out_bias, ("blk", "head"), scatter_dimension=0, tiled=True),
        lax.psum_scatter(grad_gain_one, ("blk", "head"), scatter_dimension=0, tiled=True),
        lax.psum_scatter(grad_shift_one, ("blk", "head"), scatter_dimension=0, tiled=True),
        lax.psum_scatter(grad_up_mat, ("blk", "head"), scatter_dimension=0, tiled=True),
        lax.psum_scatter(grad_up_bias, ("blk", "head"), scatter_dimension=0, tiled=True),
        lax.psum_scatter(grad_down_mat, ("blk", "head"), scatter_dimension=0, tiled=True),
        lax.psum_scatter(grad_down_bias, ("blk", "head"), scatter_dimension=0, tiled=True),
        lax.psum_scatter(grad_gain_two, ("blk", "head"), scatter_dimension=0, tiled=True),
        lax.psum_scatter(grad_shift_two, ("blk", "head"), scatter_dimension=0, tiled=True),
    )
    return (
        output,
        grad_rows.reshape(seqs, tokens, width),
        shards[0],
        shards[1],
        shards[2],
        shards[3],
        shards[4],
        shards[5],
        shards[6],
        shards[7],
        shards[8],
        shards[9],
        shards[10],
        shards[11],
        shards[12],
        shards[13],
        shards[14],
    )


def body(*args):
    hidden_in, cotangent, lengths = args[:3]
    seqs, tokens, width = hidden_in.shape
    p = Plan(
        lax.axis_size("blk"), lax.axis_size("head"), seqs, tokens, width, args[12].shape[1]
    )
    if not p.fits():
        return plain_body(*args)
    return layer(p, hidden_in, cotangent, lengths, args[3:])


def solution(mesh):
    placed = (
        P(None, ("blk", "head"), None),
        P(None, ("blk", "head"), None),
        P(),
        P(("blk", "head"), None),
        P(("blk", "head")),
        P(("blk", "head"), None),
        P(("blk", "head"), None),
        P(("blk", "head")),
        P(("blk", "head"), None),
        P(("blk", "head")),
        P(("blk", "head")),
        P(("blk", "head")),
        P(("blk", "head"), None),
        P(("blk", "head")),
        P(("blk", "head"), None),
        P(("blk", "head")),
        P(("blk", "head")),
        P(("blk", "head")),
    )
    return jax.shard_map(
        body,
        mesh=mesh,
        in_specs=placed,
        out_specs=(
            P(None, ("blk", "head"), None),
            P(None, ("blk", "head"), None),
            P(("blk", "head"), None),
            P(("blk", "head")),
            P(("blk", "head"), None),
            P(("blk", "head"), None),
            P(("blk", "head")),
            P(("blk", "head"), None),
            P(("blk", "head")),
            P(("blk", "head")),
            P(("blk", "head")),
            P(("blk", "head"), None),
            P(("blk", "head")),
            P(("blk", "head"), None),
            P(("blk", "head")),
            P(("blk", "head")),
            P(("blk", "head")),
        ),
        check_vma=False,
    )
```
